32 devices in a mesh: grp: 2 (over x), pix: 16 (over z, y, core).
Axes of the slice: x: 2, y: 2, z: 4, core: 2. Of those that a mesh axis runs over, the one named last changes fastest.
Arguments:
- spectra: float32 [224, 49152], P(None, ('grp', 'pix')), parts along dimension 1, may hold values from 0.03 to 1.2, as said below
- library: float32 [224, 240], replicated, may hold values from 0.1 to 0.5
- segment_ids: int32 [768], P(('grp', 'pix')), parts along dimension 0, may hold values from 0 to 95, never falling along the last dimension, each value on 1 to 8 neighbouring positions
- valid_mask: int32 [49152], P(('grp', 'pix')), parts along dimension 0, may hold values 0 or 1
Outputs:
- abundances: float32 [240, 49152], P(None, ('grp', 'pix')), parts along dimension 1
- new_library: float32 [448, 240], P('grp'), parts along dimension 0
The draws below stay inside these ranges and needn't reach their ends.
There are 2 independent parts, one for each index of `grp`. The reference program is written for one: setup_inputs(seed, part) draws one part's arguments, and reference() takes and returns one part's arrays. A program takes and returns all parts, laid end to end along the dimension named above; an argument that names none is the same for every part. Nothing has to cross between parts.
Inputs may be any that keep to these rules, and one draw needn't show every extreme that they name: `spectra`: positive reflectances. `segment_ids`: never falls along the strip; one segment spans 1 to 8 columns.
All inputs are finite; a program needn't handle non-finite values. No bound on the sum of `valid_mask` on one device may be relied on, other than what follows from the above.
Results may differ from the reference program's by a relative error of at most 0.0003.
Values sent between devices are 32-bit elements; how exact they have to be, the bound alone decides.
A program may use at most 64 MiB of HBM per device.

```python
import math
import jax
import jax.numpy as jnp
import numpy as np
from jax import lax

BANDS = 224
ENDM = 240
ROWS = 64
ITERS = 3
SWEEPS = 2
COLUMNS = 384
PIXELS = 24576


def draw_spectra(key, part):
    first = jax.random.fold_in(jax.random.fold_in(key, 11), 0)
    column = (jnp.arange(PIXELS, dtype=jnp.int32) // ROWS).astype(jnp.float32)
    ramp = jnp.exp(jnp.log(3.0) * column / COLUMNS)
    base = jnp.exp(jax.random.uniform(first, (BANDS, PIXELS), jnp.float32, jnp.log(0.04), jnp.log(0.4)))
    return base * ramp


def with_ends(array, stream_key, low, high):
    extent = array.shape
    spot = [jax.random.randint(jax.random.fold_in(stream_key, axis), (), 0, extent[axis]) for axis in range(len(extent))]
    array = array.at[tuple(spot)].set(low)
    longest = extent.index(max(extent))
    spot[longest] = (spot[longest] + 1) % extent[longest]
    return array.at[tuple(spot)].set(high)


def split_up(count, total, most, skew):
    loads = [(1 << 20) // math.isqrt(standing ** skew) + 1 for standing in range(2, count + 1)]
    surplus, given = total - most - (count - 1), [1] * (count - 1)
    while surplus > 0:
        free = [i for i in range(count - 1) if given[i] < most]
        mass, budget = sum([loads[i] for i in free]), surplus
        for i in free:
            more = min(most - given[i], max(1, budget * loads[i] // mass), surplus)
            given[i] = given[i] + more
            surplus = surplus - more
    return np.array([most] + given)


def uneven_parts(rng, count, total, bound, slope):
    if count == 2:
        one = jax.random.randint(rng, (), max(1, total - bound), min(bound, total - 1) + 1)
        return jnp.stack([one, total - one])
    lengths = jnp.asarray(split_up(count, total, bound, slope), jnp.int32)
    pairs = (count - 1) // 2
    giver, receiver = lengths[1:1 + 2 * pairs:2], lengths[2:2 + 2 * pairs:2]
    room = jnp.minimum(giver - 1, bound - receiver)
    moved = jax.random.randint(jax.random.fold_in(rng, 1), (pairs,), 0, 1 << 20) % (room + 1)
    lengths = lengths.at[1:1 + 2 * pairs:2].set(giver - moved).at[2:2 + 2 * pairs:2].set(receiver + moved)
    return lengths[jax.random.permutation(jax.random.fold_in(rng, 2), count)]


def setup_inputs(seed: int = 0, part: int = 0) -> dict:
    seeds = jax.random.split(jax.random.key(seed), 5)
    own_keys = jax.random.split(jax.random.fold_in(seeds[4], part), 5)
    spectra = draw_spectra(jax.random.fold_in(jax.random.fold_in(seeds[4], part), 71), part)
    library = jnp.clip(jax.random.uniform(seeds[1], (BANDS, ENDM), jnp.float32, 0.1, 0.5), 0.1, 0.5)
    segment_ids = jnp.searchsorted(jnp.cumsum(uneven_parts(own_keys[2], COLUMNS // 4, COLUMNS, 8, 0)), jnp.arange(COLUMNS), side="right").astype(jnp.int32)
    valid_mask = with_ends((jax.random.randint(own_keys[3], (PIXELS,), 0, 8) < 7).astype(jnp.int32), jax.random.fold_in(own_keys[3], 1), 0, 1)
    return {"spectra": spectra, "library": library, "segment_ids": segment_ids, "valid_mask": valid_mask}


penalty = 0.5
sparsity = 0.005
smoothness = 0.01
update_guard = 0.001
highest = lax.Precision.HIGHEST

def row_flags(span_cells):
    within = jnp.arange(span_cells, dtype=jnp.int32) % ROWS
    return ((within < ROWS - 1).astype(jnp.float32), (within > 0).astype(jnp.float32))

def jacobi_sweep(current, target, col_links):
    span_cells = current.shape[1] - 2 * ROWS
    below_on, above_on = row_flags(span_cells)
    right_on = jnp.repeat(col_links[1:], ROWS)
    left_on = jnp.repeat(col_links[:-1], ROWS)
    summed = target + below_on * current[:, ROWS + 1:ROWS + 1 + span_cells] + above_on * current[:, ROWS - 1:ROWS - 1 + span_cells] + right_on * current[:, 2 * ROWS:] + left_on * current[:, :span_cells]
    return summed / (1.0 + below_on + above_on + right_on + left_on)

def differences(current, right_links):
    span_cells = current.shape[1] - ROWS
    below_on, above_on = row_flags(span_cells)
    vertical = below_on * (current[:, 1:span_cells + 1] - current[:, :span_cells])
    horizontal = jnp.repeat(right_links, ROWS) * (current[:, ROWS:] - current[:, :span_cells])
    return jnp.stack([vertical, horizontal])

def adjoint(dual_sum, left_edge, col_links):
    span_cells = dual_sum.shape[2]
    below_on, above_on = row_flags(span_cells)
    down_part = below_on * dual_sum[0]
    across = jnp.repeat(col_links[1:], ROWS) * dual_sum[1]
    shifted_down = jnp.concatenate([jnp.zeros_like(down_part[:, :1]), down_part[:, :-1]], axis=1)
    shifted_across = jnp.concatenate([col_links[0] * left_edge, across[:, :-ROWS]], axis=1)
    return shifted_down - down_part + shifted_across - across

def apply_inverse(factor, right_side):
    return jax.scipy.linalg.cho_solve((factor, True), right_side)

def reference(spectra, library, segment_ids, valid_mask):
    members = library.shape[1]
    system = jnp.dot(library.T, library, precision=highest) + 2.0 * jnp.eye(members, dtype=jnp.float32)
    factor = jnp.linalg.cholesky(system)
    valid_cells = valid_mask.astype(jnp.float32)
    same_next = (segment_ids[:-1] == segment_ids[1:]).astype(jnp.float32)
    zero_link = jnp.zeros((1,), jnp.float32)
    col_links = jnp.concatenate([zero_link, same_next, zero_link])
    zeros_field = jnp.zeros((members, PIXELS), jnp.float32)
    zero_edge = jnp.zeros((members, ROWS), jnp.float32)
    fitted = spectra
    smooth = zeros_field
    sparse = zeros_field
    dual_fit = jnp.zeros_like(spectra)
    dual_smooth = zeros_field
    dual_sparse = zeros_field
    edge_vars = jnp.zeros((2, members, PIXELS), jnp.float32)
    dual_edges = edge_vars
    for iteration in range(ITERS):
        right_side = jnp.dot(library.T, fitted + dual_fit, precision=highest) + smooth + dual_smooth + sparse + dual_sparse
        unmixed = apply_inverse(factor, right_side)
        model_fit = jnp.dot(library, unmixed, precision=highest)
        fitted = (valid_cells * spectra + penalty * (model_fit - dual_fit)) / (valid_cells + penalty)
        sparse = jnp.maximum(unmixed - dual_sparse - sparsity / penalty, 0.0)
        target = unmixed - dual_smooth + adjoint(edge_vars + dual_edges, zero_edge, col_links)
        for sweep_index in range(SWEEPS):
            padded = jnp.concatenate([zero_edge, smooth, zero_edge], axis=1)
            smooth = jacobi_sweep(padded, target, col_links)
        extended = jnp.concatenate([smooth, zero_edge], axis=1)
        change = differences(extended, col_links[1:])
        shrunk = change - dual_edges
        edge_vars = shrunk - jnp.clip(shrunk, -smoothness / penalty, smoothness / penalty)
        dual_edges = dual_edges - (change - edge_vars)
        dual_fit = dual_fit - (model_fit - fitted)
        dual_smooth = dual_smooth - (unmixed - smooth)
        dual_sparse = dual_sparse - (unmixed - sparse)
    right_side = jnp.dot(library.T, fitted + dual_fit, precision=highest) + smooth + dual_smooth + sparse + dual_sparse
    unmixed = apply_inverse(factor, right_side)
    abundances = jnp.maximum(unmixed - dual_sparse - sparsity / penalty, 0.0)
    contract = (((1,), (1,)), ((), ()))
    numerator = lax.dot_general(spectra * valid_cells, abundances, contract, precision=highest) / PIXELS
    gram_total = lax.dot_general(abundances * valid_cells, abundances, contract, precision=highest) / PIXELS
    denominator = jnp.dot(library, gram_total, precision=highest)
    new_library = library * (numerator + update_guard) / (denominator + update_guard)
    return (abundances, new_library)
```

```python
import functools

import jax
import jax.numpy as jnp
from jax import lax
from jax.experimental import pallas as pl
from jax.experimental.pallas import tpu as pltpu
from jax.sharding import PartitionSpec as P

ROWS = 64
ITERS = 3
SWEEPS = 2
HALO = 2 * ITERS
LANES = 128
CHUNK = 256

penalty = 0.5
sparsity = 0.005
smoothness = 0.01
update_guard = 0.001
highest = lax.Precision.HIGHEST
SQUARINGS = 8
REFINES = 1
VMEM_LIMIT = 60000 * 1024


def matmul(a, b):
    return jnp.dot(a, b, precision=highest, preferred_element_type=jnp.float32)


def matmul_nt(a, b):
    return lax.dot_general(
        a, b, (((1,), (1,)), ((), ())), precision=highest, preferred_element_type=jnp.float32
    )


def matmul_tn(a, b):
    return lax.dot_general(
        a, b, (((0,), (0,)), ((), ())), precision=highest, preferred_element_type=jnp.float32
    )


def inverse_kernel(lib_ref, gain_ref, inv_ref):
    lib = lib_ref[...]
    n = lib.shape[1]
    rows = lax.broadcasted_iota(jnp.int32, (n, n), 0)
    cols = lax.broadcasted_iota(jnp.int32, (n, n), 1)
    eye = (rows == cols).astype(jnp.float32)
    system = matmul_tn(lib, lib) + 2.0 * eye
    bound = jnp.max(jnp.sum(jnp.abs(system), axis=1, keepdims=True), axis=0, keepdims=True)
    scale = 2.0 / (bound + 2.0)
    r = (bound - 2.0) / (bound + 2.0)
    resid = eye - scale * system
    approx = scale * eye
    for step in range(SQUARINGS):
        s = 2.0 / (2.0 - r * r)
        if step == 0:
            approx = (s * scale) * (eye + resid)
            resid = (1.0 - s) * eye + s * matmul(resid, resid)
        elif step < SQUARINGS - 1:
            both = matmul(jnp.concatenate([approx, resid], axis=0), resid)
            approx = s * (approx + both[:n])
            resid = (1.0 - s) * eye + s * both[n:]
        else:
            approx = s * (approx + matmul(approx, resid))
        r = r * r / (2.0 - r * r)
    for _ in range(REFINES):
        resid = eye - matmul(approx, system)
        approx = approx + matmul(resid, approx)
    inv_ref[...] = approx
    gain_ref[...] = matmul_nt(approx, lib)


def admm_kernel(
    total_pixels,
    spec_ref, left_ref, right_ref, aux_ref, lib_ref, gain_ref, inv_ref,
    abund_ref, sums_ref,
    s_ref, v_ref, d1_ref, w_ref, x_ref, v2_ref, d2_ref, e_ref, d4_ref, cv_ref, ch_ref,
    valid_ref, rinv_ref, lr_ref, ll_ref, count_ref,
):
    bands, here = spec_ref.shape
    members = lib_ref.shape[1]
    side = left_ref.shape[1]
    wide = here + 2 * side
    s_ref[:, 0:side] = left_ref[...]
    s_ref[:, side : side + here] = spec_ref[...]
    s_ref[:, side + here : wide] = right_ref[...]
    lane = lax.broadcasted_iota(jnp.int32, (8, LANES), 1)
    within = lane % ROWS
    below = (within < ROWS - 1).astype(jnp.float32)
    above = (within > 0).astype(jnp.float32)
    first_half = lane < ROWS
    tiles_all = wide // LANES

    def at(ref, i, rows=slice(0, 8)):
        return ref[rows, i * LANES : (i + 1) * LANES]

    segs = [jnp.broadcast_to(aux_ref[1:2, i * LANES : (i + 1) * LANES], (8, LANES)) for i in range(tiles_all)]
    rolled = [pltpu.roll(t, ROWS, 1) for t in segs]
    for i in range(tiles_all):
        right = jnp.where(first_half, rolled[i], rolled[min(i + 1, tiles_all - 1)])
        left = jnp.where(first_half, rolled[max(i - 1, 0)], rolled[i])
        lr = (right == segs[i]).astype(jnp.float32)
        ll = (left == segs[i]).astype(jnp.float32)
        sl = slice(i * LANES, (i + 1) * LANES)
        lr_ref[:, sl] = lr
        ll_ref[:, sl] = ll
        count_ref[:, sl] = 1.0 / (1.0 + below + above + lr + ll)
        ok = jnp.broadcast_to(aux_ref[0:1, sl], (8, LANES))
        valid_ref[:, sl] = ok
        rinv_ref[:, sl] = 1.0 / (ok + penalty)

    lib = lib_ref[...]
    cut = smoothness / penalty
    thresh = sparsity / penalty

    for it in range(ITERS):
        final_turn = it == ITERS - 1
        lo = it * LANES
        span = wide - 2 * lo

        def mix(k, carry, it=it, lo=lo):
            cells = pl.ds(pl.multiple_of(lo + k * CHUNK, LANES), CHUNK)
            spec = s_ref[:, cells]
            if it == 0:
                x = matmul(gain_ref[...], spec)
            else:
                x = matmul(gain_ref[...], v_ref[:, cells]) + matmul(inv_ref[...], w_ref[:, cells])
            x_ref[:, cells] = x
            g = matmul(lib, x)
            if it > 0:
                g = g - d1_ref[:, cells]
            v1 = (valid_ref[0:1, cells] * spec + penalty * g) * rinv_ref[0:1, cells]
            d1 = v1 - g
            if not final_turn:
                d1_ref[:, cells] = d1
            v_ref[:, cells] = v1 + d1
            return carry

        lax.fori_loop(0, span // CHUNK, mix, 0)

        first, last = lo // LANES, (wide - lo) // LANES

        def smooth_rows(b, carry, it=it, first=first, last=last, final_turn=final_turn):
            rows = pl.ds(pl.multiple_of(b * 8, 8), 8)

            def tile(ref, i):
                return ref[rows, i * LANES : (i + 1) * LANES]

            def put(ref, i, value):
                ref[rows, i * LANES : (i + 1) * LANES] = value

            def clamp(i):
                return min(max(i, first), last - 1)

            def half_rolled(field):
                return functools.cache(lambda i: pltpu.roll(field(i), ROWS, 1))

            def neighbours(field, half, i):
                mine = field(i)
                total = below * pltpu.roll(mine, LANES - 1, 1) + above * pltpu.roll(mine, 1, 1)
                total += at(lr_ref, i) * jnp.where(first_half, half(i), half(clamp(i + 1)))
                total += at(ll_ref, i) * jnp.where(first_half, half(clamp(i - 1)), half(i))
                return total

            @functools.cache
            def x(i):
                return tile(x_ref, i)

            @functools.cache
            def target(i):
                return x(i) if it == 0 else x(i) + tile(e_ref, i)

            if it > 0:
                @functools.cache
                def before(i):
                    return tile(v2_ref, i)

                before_half = half_rolled(before)

            @functools.cache
            def once(i):
                if it == 0:
                    return target(i) * at(count_ref, i)
                return (target(i) + neighbours(before, before_half, i)) * at(count_ref, i)

            once_half = half_rolled(once)

            @functools.cache
            def twice(i):
                return (target(i) + neighbours(once, once_half, i)) * at(count_ref, i)

            twice_half = half_rolled(twice)

            @functools.cache
            def edges(i):
                mine = twice(i)
                sv = below * (pltpu.roll(mine, LANES - 1, 1) - mine)
                sh = at(lr_ref, i) * (
                    jnp.where(first_half, twice_half(i), twice_half(clamp(i + 1))) - mine
                )
                if it > 0:
                    sv += tile(cv_ref, i)
                    sh += tile(ch_ref, i)
                cv = jnp.clip(sv, -cut, cut)
                ch = jnp.clip(sh, -cut, cut)
                return sv - 2.0 * cv, sh - 2.0 * ch, cv, ch

            dual_half = functools.cache(lambda i: pltpu.roll(edges(i)[1], ROWS, 1))

            for i in range(first, last):
                v2 = twice(i)
                d2 = v2 - x(i)
                if it > 0:
                    d2 += tile(d2_ref, i)
                part = x(i) if it == 0 else x(i) - tile(d4_ref, i)
                v4 = jnp.maximum(part - thresh, 0.0)
                d4 = v4 - part
                put(w_ref, i, (v2 + d2) + (v4 + d4))
                put(d4_ref, i, d4)
                if not final_turn:
                    wv, wh, cv, ch = edges(i)
                    across = jnp.where(first_half, dual_half(clamp(i - 1)), dual_half(i))
                    put(e_ref, i, (pltpu.roll(wv, 1, 1) - wv) + (across - wh) - d2)
                    put(d2_ref, i, d2)
                    put(cv_ref, i, cv)
                    put(ch_ref, i, ch)
            if not final_turn:
                for i in range(first, last):
                    put(v2_ref, i, twice(i))
            return carry

        lax.fori_loop(0, members // 8, smooth_rows, 0)

    def finish(k, carry):
        cells = pl.ds(pl.multiple_of(side + k * CHUNK, LANES), CHUNK)
        out = pl.ds(pl.multiple_of(k * CHUNK, LANES), CHUNK)
        x = matmul(gain_ref[...], v_ref[:, cells]) + matmul(inv_ref[...], w_ref[:, cells])
        abund = jnp.maximum(x - d4_ref[:, cells] - thresh, 0.0)
        abund_ref[:, out] = abund
        ok = valid_ref[0:1, cells]
        masked = abund * ok
        numer = matmul_nt(s_ref[:, cells] * ok, abund)
        gram = matmul_nt(masked, abund)
        sums_ref[0:bands, :] += numer
        sums_ref[bands:, :] += gram
        return carry

    sums_ref[...] = jnp.zeros_like(sums_ref)
    lax.fori_loop(0, here // CHUNK, finish, 0)
    sums_ref[...] = sums_ref[...] * (1.0 / total_pixels)


def on_device(spectra, library, segment_ids, valid_mask):
    peers = lax.axis_size("pix")
    bands, here = spectra.shape
    members = library.shape[1]
    side = HALO * ROWS
    wide = here + 2 * side
    up = [(i, i + 1) for i in range(peers - 1)]
    down = [(i + 1, i) for i in range(peers - 1)]
    marked = jnp.repeat((segment_ids + 1).astype(jnp.float32), ROWS)
    aux = jnp.stack([valid_mask.astype(jnp.float32), marked])
    left = lax.ppermute(spectra[:, here - side :], "pix", up)
    right = lax.ppermute(spectra[:, :side], "pix", down)
    aux_left = lax.ppermute(aux[:, here - side :], "pix", up)
    aux_right = lax.ppermute(aux[:, :side], "pix", down)
    aux = jnp.concatenate([aux_left, aux, aux_right], axis=1)
    vmem = pl.BlockSpec(memory_space=pltpu.VMEM)
    gain, inverse = pl.pallas_call(
        inverse_kernel,
        out_shape=(
            jax.ShapeDtypeStruct((members, bands), jnp.float32),
            jax.ShapeDtypeStruct((members, members), jnp.float32),
        ),
        in_specs=[vmem],
        out_specs=(vmem, vmem),
        name="inverse",
    )(library)
    field = pltpu.VMEM((members, wide), jnp.float32)
    band_field = pltpu.VMEM((bands, wide), jnp.float32)
    line = pltpu.VMEM((8, wide), jnp.float32)
    abundances, sums = pl.pallas_call(
        functools.partial(admm_kernel, here * peers),
        out_shape=(
            jax.ShapeDtypeStruct((members, here), jnp.float32),
            jax.ShapeDtypeStruct((bands + members, members), jnp.float32),
        ),
        in_specs=[vmem] * 7,
        out_specs=(vmem, vmem),
        scratch_shapes=[band_field] * 3 + [field] * 8 + [line] * 5,
        compiler_params=pltpu.CompilerParams(vmem_limit_bytes=VMEM_LIMIT),
        name="admm",
    )(spectra, left, right, aux, library, gain, inverse)
    sums = lax.psum(sums, "pix")
    denominator = jnp.dot(library, sums[bands:], precision=highest)
    new_library = library * (sums[:bands] + update_guard) / (denominator + update_guard)
    return (abundances, new_library)


def solution(mesh):
    placed = (P(None, ("grp", "pix")), P(), P(("grp", "pix")), P(("grp", "pix")))
    return jax.shard_map(
        on_device,
        mesh=mesh,
        in_specs=placed,
        out_specs=(P(None, ("grp", "pix")), P("grp", None)),
        check_vma=False,
    )
```

```python
import functools

import jax
import jax.numpy as jnp
from jax import lax
from jax.experimental import pallas as pl
from jax.experimental.pallas import tpu as pltpu
from jax.sharding import PartitionSpec as P

ROWS = 64
ITERS = 3
SWEEPS = 2
HALO = 2 * ITERS
LANES = 128
CHUNK = 256

penalty = 0.5
sparsity = 0.005
smoothness = 0.01
update_guard = 0.001
highest = lax.Precision.HIGHEST
SQUARINGS = 8
REFINES = 1
VMEM_LIMIT = 60000 * 1024


def matmul(a, b):
    return jnp.dot(a, b, precision=highest, preferred_element_type=jnp.float32)


def matmul_nt(a, b):
    return lax.dot_general(
        a, b, (((1,), (1,)), ((), ())), precision=highest, preferred_element_type=jnp.float32
    )


def matmul_tn(a, b):
    return lax.dot_general(
        a, b, (((0,), (0,)), ((), ())), precision=highest, preferred_element_type=jnp.float32
    )


def split(a):
    high = a.astype(jnp.bfloat16)
    return high, (a - high.astype(jnp.float32)).astype(jnp.bfloat16)


def matmul_split(a_ref, b):
    high, low = split(b)
    product = functools.partial(jnp.dot, preferred_element_type=jnp.float32)
    depth = b.shape[0]
    a_high, a_low = a_ref[0, :, 0:depth], a_ref[1, :, 0:depth]
    return product(a_high, high) + (product(a_high, low) + product(a_low, high))


def matmul_nt_split(a, b):
    contract = (((1,), (1,)), ((), ()))
    product = functools.partial(
        lax.dot_general, dimension_numbers=contract, preferred_element_type=jnp.float32
    )
    (a_high, a_low), (b_high, b_low) = split(a), split(b)
    return product(a_high, b_high) + (product(a_high, b_low) + product(a_low, b_high))


def inverse_kernel(lib_ref, solve_ref, split_lib_ref):
    lib = lib_ref[...]
    n = lib.shape[1]
    rows = lax.broadcasted_iota(jnp.int32, (n, n), 0)
    cols = lax.broadcasted_iota(jnp.int32, (n, n), 1)
    eye = (rows == cols).astype(jnp.float32)
    system = matmul_tn(lib, lib) + 2.0 * eye
    bound = jnp.max(jnp.sum(jnp.abs(system), axis=1, keepdims=True), axis=0, keepdims=True)
    scale = 2.0 / (bound + 2.0)
    r = (bound - 2.0) / (bound + 2.0)
    resid = eye - scale * system
    approx = scale * eye
    for step in range(SQUARINGS):
        s = 2.0 / (2.0 - r * r)
        if step == 0:
            approx = (s * scale) * (eye + resid)
            resid = (1.0 - s) * eye + s * matmul(resid, resid)
        elif step < SQUARINGS - 1:
            both = matmul(jnp.concatenate([approx, resid], axis=0), resid)
            approx = s * (approx + both[:n])
            resid = (1.0 - s) * eye + s * both[n:]
        else:
            approx = s * (approx + matmul(approx, resid))
        r = r * r / (2.0 - r * r)
    for _ in range(REFINES):
        resid = eye - matmul(approx, system)
        approx = approx + matmul(resid, approx)
    bands = lib.shape[0]
    high, low = split(matmul_nt(approx, lib))
    solve_ref[0, :, 0:bands] = high
    solve_ref[1, :, 0:bands] = low
    high, low = split(approx)
    solve_ref[0, :, bands:] = high
    solve_ref[1, :, bands:] = low
    high, low = split(lib)
    split_lib_ref[0] = high
    split_lib_ref[1] = low


def admm_kernel(
    padded_bands,
    spec_ref, left_ref, right_ref, aux_ref, solve_ref, split_lib_ref,
    abund_ref, sums_ref,
    s_ref, vw_ref, d1_ref, x_ref, v2_ref, d2_ref, e_ref, d4_ref, cv_ref, ch_ref,
    valid_ref, rinv_ref, lr_ref, ll_ref, count_ref,
):
    bands, here = spec_ref.shape
    members = split_lib_ref.shape[2]
    side = left_ref.shape[1]
    wide = here + 2 * side
    s_ref[:, 0:side] = left_ref[...]
    s_ref[:, side : side + here] = spec_ref[...]
    s_ref[:, side + here : wide] = right_ref[...]
    lane = lax.broadcasted_iota(jnp.int32, (8, LANES), 1)
    within = lane % ROWS
    below = (within < ROWS - 1).astype(jnp.float32)
    above = (within > 0).astype(jnp.float32)
    first_half = lane < ROWS
    tiles_all = wide // LANES

    def at(ref, i, rows=slice(0, 8)):
        return ref[rows, i * LANES : (i + 1) * LANES]

    segs = [jnp.broadcast_to(aux_ref[1:2, i * LANES : (i + 1) * LANES], (8, LANES)) for i in range(tiles_all)]
    rolled = [pltpu.roll(t, ROWS, 1) for t in segs]
    for i in range(tiles_all):
        right = jnp.where(first_half, rolled[i], rolled[min(i + 1, tiles_all - 1)])
        left = jnp.where(first_half, rolled[max(i - 1, 0)], rolled[i])
        lr = (right == segs[i]).astype(jnp.float32)
        ll = (left == segs[i]).astype(jnp.float32)
        sl = slice(i * LANES, (i + 1) * LANES)
        lr_ref[:, sl] = lr
        ll_ref[:, sl] = ll
        count_ref[:, sl] = 1.0 / (1.0 + below + above + lr + ll)
        ok = jnp.broadcast_to(aux_ref[0:1, sl], (8, LANES))
        valid_ref[:, sl] = ok
        rinv_ref[:, sl] = 1.0 / (ok + penalty)

    cut = smoothness / penalty
    thresh = sparsity / penalty

    for it in range(ITERS):
        final_turn = it == ITERS - 1
        lo = it * LANES
        span = wide - 2 * lo

        def mix(k, carry, it=it, lo=lo):
            cells = pl.ds(pl.multiple_of(lo + k * CHUNK, LANES), CHUNK)
            spec = s_ref[:, cells]
            if it == 0:
                x = matmul_split(solve_ref, spec)
            else:
                x = matmul_split(solve_ref, vw_ref[:, cells])
            x_ref[:, cells] = x
            g = matmul_split(split_lib_ref, x)
            if it > 0:
                g = g - d1_ref[:, cells]
            v1 = (valid_ref[0:1, cells] * spec + penalty * g) * rinv_ref[0:1, cells]
            d1 = v1 - g
            if not final_turn:
                d1_ref[:, cells] = d1
            vw_ref[0:bands, cells] = v1 + d1
            return carry

        lax.fori_loop(0, span // CHUNK, mix, 0)

        first, last = lo // LANES, (wide - lo) // LANES

        def smooth_rows(b, carry, it=it, first=first, last=last, final_turn=final_turn):
            rows = pl.ds(pl.multiple_of(b * 8, 8), 8)
            wrows = pl.ds(pl.multiple_of(bands + b * 8, 8), 8)

            def tile(ref, i):
                return ref[rows, i * LANES : (i + 1) * LANES]

            def put(ref, i, value):
                ref[rows, i * LANES : (i + 1) * LANES] = value

            def clamp(i):
                return min(max(i, first), last - 1)

            def half_rolled(field):
                return functools.cache(lambda i: pltpu.roll(field(i), ROWS, 1))

            def neighbours(field, half, i):
                mine = field(i)
                total = below * pltpu.roll(mine, LANES - 1, 1) + above * pltpu.roll(mine, 1, 1)
                total += at(lr_ref, i) * jnp.where(first_half, half(i), half(clamp(i + 1)))
                total += at(ll_ref, i) * jnp.where(first_half, half(clamp(i - 1)), half(i))
                return total

            @functools.cache
            def x(i):
                return tile(x_ref, i)

            @functools.cache
            def target(i):
                return x(i) if it == 0 else x(i) + tile(e_ref, i)

            if it > 0:
                @functools.cache
                def before(i):
                    return tile(v2_ref, i)

                before_half = half_rolled(before)

            @functools.cache
            def once(i):
                if it == 0:
                    return target(i) * at(count_ref, i)
                return (target(i) + neighbours(before, before_half, i)) * at(count_ref, i)

            once_half = half_rolled(once)

            @functools.cache
            def twice(i):
                return (target(i) + neighbours(once, once_half, i)) * at(count_ref, i)

            twice_half = half_rolled(twice)

            @functools.cache
            def edges(i):
                mine = twice(i)
                sv = below * (pltpu.roll(mine, LANES - 1, 1) - mine)
                sh = at(lr_ref, i) * (
                    jnp.where(first_half, twice_half(i), twice_half(clamp(i + 1))) - mine
                )
                if it > 0:
                    sv += tile(cv_ref, i)
                    sh += tile(ch_ref, i)
                cv = jnp.clip(sv, -cut, cut)
                ch = jnp.clip(sh, -cut, cut)
                return sv - 2.0 * cv, sh - 2.0 * ch, cv, ch

            dual_half = functools.cache(lambda i: pltpu.roll(edges(i)[1], ROWS, 1))

            for i in range(first, last):
                v2 = twice(i)
                d2 = v2 - x(i)
                if it > 0:
                    d2 += tile(d2_ref, i)
                part = x(i) if it == 0 else x(i) - tile(d4_ref, i)
                v4 = jnp.maximum(part - thresh, 0.0)
                d4 = v4 - part
                vw_ref[wrows, i * LANES : (i + 1) * LANES] = (v2 + d2) + (v4 + d4)
                put(d4_ref, i, d4)
                if not final_turn:
                    wv, wh, cv, ch = edges(i)
                    across = jnp.where(first_half, dual_half(clamp(i - 1)), dual_half(i))
                    put(e_ref, i, (pltpu.roll(wv, 1, 1) - wv) + (across - wh) - d2)
                    put(d2_ref, i, d2)
                    put(cv_ref, i, cv)
                    put(ch_ref, i, ch)
            if not final_turn:
                for i in range(first, last):
                    put(v2_ref, i, twice(i))
            return carry

        lax.fori_loop(0, members // 8, smooth_rows, 0)

    def finish(k, carry):
        cells = pl.ds(pl.multiple_of(side + k * CHUNK, LANES), CHUNK)
        out = pl.ds(pl.multiple_of(k * CHUNK, LANES), CHUNK)
        x = matmul_split(solve_ref, vw_ref[:, cells])
        abund = jnp.maximum(x - d4_ref[:, cells] - thresh, 0.0)
        abund_ref[:, out] = abund
        masked = abund * valid_ref[0:1, cells]
        sums_ref[0:members, 0:bands] += matmul_nt_split(masked, s_ref[:, cells])
        sums_ref[0:members, padded_bands : padded_bands + members] += matmul_nt_split(masked, abund)
        return carry

    sums_ref[...] = jnp.zeros_like(sums_ref)
    lax.fori_loop(0, here // CHUNK, finish, 0)


def total_kernel(
    total_pixels, bands, members, per, groups,
    part_ref, lib_ref, turned_ref, out_ref,
    pair_ref, acc_ref, got_ref, rows_ref,
    pair_send, pair_recv, sum_send, sum_recv, row_send, row_recv, swap_send, swap_recv,
):
    me = lax.axis_index("pix")
    core = me % 2
    spot = me // 2
    half = per * groups
    wide = rows_ref.shape[1]
    partner = {"pix": spot * 2 + 1 - core}

    def peer(k):
        return {"pix": ((spot + k) % groups) * 2 + core}

    barrier = pltpu.get_barrier_semaphore()
    pl.semaphore_signal(barrier, inc=1, device_id=partner)
    for k in range(1, groups):
        pl.semaphore_signal(barrier, inc=1, device_id=peer(k))
    pl.semaphore_wait(barrier, groups)

    def block(k, of_core):
        place = of_core * half + ((spot + k) % groups) * per
        return pl.ds(pl.multiple_of(place, per), per)

    order = list(range(1, groups)) + [0]
    pair_copies = {}
    for k in order:
        pair_copies[k] = pltpu.make_async_remote_copy(
            part_ref.at[block(k, 1 - core)], pair_ref.at[k], pair_send.at[k], pair_recv.at[k],
            device_id=partner,
        )
        pair_copies[k].start()
    sum_copies = {}
    for k in order:
        pair_copies[k].wait_recv()
        acc_ref[k] = part_ref[block(k, core), :] + pair_ref[k]
        if k > 0:
            sum_copies[k] = pltpu.make_async_remote_copy(
                acc_ref.at[k], got_ref.at[k], sum_send.at[k], sum_recv.at[k], device_id=peer(k)
            )
            sum_copies[k].start()
    total = acc_ref[0]
    for k in range(1, groups):
        sum_copies[k].wait_recv()
        total += got_ref[k]
    total = total * (1.0 / total_pixels)
    mine = block(0, core)
    gram = total[:, wide : wide + members]
    denominator = matmul_nt(gram, lib_ref[...])
    rows_ref[mine, :] = jnp.zeros((per, wide), jnp.float32)
    rows_ref[mine, 0:bands] = (
        turned_ref[mine, :] * (total[:, 0:bands] + update_guard) / (denominator + update_guard)
    )
    row_copies = {}
    for k in range(1, groups):
        row_copies[k] = pltpu.make_async_remote_copy(
            rows_ref.at[mine], rows_ref.at[mine], row_send.at[k], row_recv.at[k], device_id=peer(k)
        )
        row_copies[k].start()
    swap_copies = {}
    for k in range(groups):
        if k > 0:
            row_copies[k].wait_recv()
        there = block(-k, core)
        swap_copies[k] = pltpu.make_async_remote_copy(
            rows_ref.at[there], rows_ref.at[there], swap_send.at[k], swap_recv.at[k],
            device_id=partner,
        )
        swap_copies[k].start()
    for k in range(groups):
        swap_copies[k].wait_recv()
    out_ref[...] = rows_ref[...].T[0:bands, 0:members]
    for k in range(groups):
        pair_copies[k].wait_send()
        swap_copies[k].wait_send()
        if k > 0:
            sum_copies[k].wait_send()
            row_copies[k].wait_send()


def on_device(spectra, library, segment_ids, valid_mask):
    peers = lax.axis_size("pix")
    bands, here = spectra.shape
    members = library.shape[1]
    side = HALO * ROWS
    wide = here + 2 * side
    up = [(i, i + 1) for i in range(peers - 1)]
    down = [(i + 1, i) for i in range(peers - 1)]
    marked = jnp.repeat((segment_ids + 1).astype(jnp.float32), ROWS)
    aux = jnp.stack([valid_mask.astype(jnp.float32), marked])
    left = lax.ppermute(spectra[:, here - side :], "pix", up)
    right = lax.ppermute(spectra[:, :side], "pix", down)
    aux_left = lax.ppermute(aux[:, here - side :], "pix", up)
    aux_right = lax.ppermute(aux[:, :side], "pix", down)
    aux = jnp.concatenate([aux_left, aux, aux_right], axis=1)
    vmem = pl.BlockSpec(memory_space=pltpu.VMEM)
    solve, split_lib = pl.pallas_call(
        inverse_kernel,
        out_shape=(
            jax.ShapeDtypeStruct((2, members, bands + members), jnp.bfloat16),
            jax.ShapeDtypeStruct((2, bands, members), jnp.bfloat16),
        ),
        in_specs=[vmem],
        out_specs=(vmem, vmem),
        name="inverse",
    )(library)
    groups = peers // 2
    per = 8 * pl.cdiv(members, 8 * peers)
    padded_bands = LANES * pl.cdiv(bands, LANES)
    padded = padded_bands + LANES * pl.cdiv(members, LANES)
    field = pltpu.VMEM((members, wide), jnp.float32)
    band_field = pltpu.VMEM((bands, wide), jnp.float32)
    line = pltpu.VMEM((8, wide), jnp.float32)
    stacked = pltpu.VMEM((bands + members, wide), jnp.float32)
    scratch = [band_field, stacked, band_field] + [field] * 7 + [line] * 5
    abundances, sums = pl.pallas_call(
        functools.partial(admm_kernel, padded_bands),
        out_shape=(
            jax.ShapeDtypeStruct((members, here), jnp.float32),
            jax.ShapeDtypeStruct((per * peers, padded), jnp.float32),
        ),
        in_specs=[vmem] * 6,
        out_specs=(vmem, vmem),
        scratch_shapes=scratch,
        compiler_params=pltpu.CompilerParams(vmem_limit_bytes=VMEM_LIMIT),
        name="admm",
    )(spectra, left, right, aux, solve, split_lib)
    turned = jnp.pad(library.T, ((0, per * peers - members), (0, 0)))
    blocks = pltpu.VMEM((groups, per, padded), jnp.float32)
    new_library = pl.pallas_call(
        functools.partial(total_kernel, here * peers, bands, members, per, groups),
        out_shape=jax.ShapeDtypeStruct((bands, members), jnp.float32),
        in_specs=[vmem] * 3,
        out_specs=vmem,
        scratch_shapes=[blocks] * 3
        + [pltpu.VMEM((per * peers, padded_bands), jnp.float32)]
        + [pltpu.SemaphoreType.DMA((groups,))] * 8,
        compiler_params=pltpu.CompilerParams(collective_id=0, has_side_effects=True),
        name="total",
    )(sums, library, turned)
    return (abundances, new_library)


def solution(mesh):
    placed = (P(None, ("grp", "pix")), P(), P(("grp", "pix")), P(("grp", "pix")))
    return jax.shard_map(
        on_device,
        mesh=mesh,
        in_specs=placed,
        out_specs=(P(None, ("grp", "pix")), P("grp", None)),
        check_vma=False,
    )
```

```python
import functools

import jax
import jax.numpy as jnp
from jax import lax
from jax.experimental import pallas as pl
from jax.experimental.pallas import tpu as pltpu
from jax.sharding import PartitionSpec as P

ROWS = 64
ITERS = 3
SWEEPS = 2
HALO = 2 * ITERS
LANES = 128
CHUNK = 256
ROW_BLOCK = 8

penalty = 0.5
sparsity = 0.005
smoothness = 0.01
update_guard = 0.001
highest = lax.Precision.HIGHEST
SQUARINGS = 8
REFINES = 1
VMEM_LIMIT = 60000 * 1024


def matmul(a, b):
    return jnp.dot(a, b, precision=highest, preferred_element_type=jnp.float32)


def matmul_nt(a, b):
    return lax.dot_general(
        a, b, (((1,), (1,)), ((), ())), precision=highest, preferred_element_type=jnp.float32
    )


def matmul_tn(a, b):
    return lax.dot_general(
        a, b, (((0,), (0,)), ((), ())), precision=highest, preferred_element_type=jnp.float32
    )


def split(a):
    high = a.astype(jnp.bfloat16)
    return high, (a - high.astype(jnp.float32)).astype(jnp.bfloat16)


def matmul_split(a_ref, b):
    high, low = split(b)
    product = functools.partial(jnp.dot, preferred_element_type=jnp.float32)
    depth = b.shape[0]
    a_high, a_low = a_ref[0, :, 0:depth], a_ref[1, :, 0:depth]
    return product(a_high, high) + (product(a_high, low) + product(a_low, high))


def matmul_nt_split(a, b):
    contract = (((1,), (1,)), ((), ()))
    product = functools.partial(
        lax.dot_general, dimension_numbers=contract, preferred_element_type=jnp.float32
    )
    (a_high, a_low), (b_high, b_low) = split(a), split(b)
    return product(a_high, b_high) + (product(a_high, b_low) + product(a_low, b_high))


def start_kernel(
    peers,
    lib_ref, spec_ref, aux_ref,
    solve_ref, split_lib_ref, turned_ref, left_ref, right_ref, aux_wide_ref,
    send, recv, local,
):
    me = lax.axis_index("pix")
    here = spec_ref.shape[1]
    side = left_ref.shape[1]
    has_left, has_right = me > 0, me < peers - 1
    to_left, to_right = {"pix": me - 1}, {"pix": me + 1}

    barrier = pltpu.get_barrier_semaphore()

    @pl.when(has_left)
    def _():
        pl.semaphore_signal(barrier, inc=1, device_id=to_left)

    @pl.when(has_right)
    def _():
        pl.semaphore_signal(barrier, inc=1, device_id=to_right)

    pl.semaphore_wait(barrier, has_left.astype(jnp.int32) + has_right.astype(jnp.int32))

    heads = [
        pltpu.make_async_remote_copy(src, dst, send.at[k], recv.at[k], device_id=to_left)
        for k, (src, dst) in enumerate((
            (spec_ref.at[:, 0:side], right_ref),
            (aux_ref.at[:, 0:side], aux_wide_ref.at[:, side + here : here + 2 * side]),
        ))
    ]
    tails = [
        pltpu.make_async_remote_copy(src, dst, send.at[k + 2], recv.at[k + 2], device_id=to_right)
        for k, (src, dst) in enumerate((
            (spec_ref.at[:, here - side :], left_ref),
            (aux_ref.at[:, here - side :], aux_wide_ref.at[:, 0:side]),
        ))
    ]
    fill_left = pltpu.make_async_copy(spec_ref.at[:, 0:side], left_ref, local.at[0])
    fill_right = pltpu.make_async_copy(spec_ref.at[:, 0:side], right_ref, local.at[1])

    @pl.when(has_left)
    def _():
        for copy in heads:
            copy.start()

    @pl.when(has_right)
    def _():
        for copy in tails:
            copy.start()

    @pl.when(jnp.logical_not(has_left))
    def _():
        aux_wide_ref[:, 0:side] = jnp.zeros((8, side), jnp.float32)
        fill_left.start()

    @pl.when(jnp.logical_not(has_right))
    def _():
        aux_wide_ref[:, side + here :] = jnp.zeros((8, side), jnp.float32)
        fill_right.start()

    aux_wide_ref[:, side : side + here] = aux_ref[...]
    lib = lib_ref[...]
    n = lib.shape[1]
    rows = lax.broadcasted_iota(jnp.int32, (n, n), 0)
    cols = lax.broadcasted_iota(jnp.int32, (n, n), 1)
    eye = (rows == cols).astype(jnp.float32)
    system = matmul_tn(lib, lib) + 2.0 * eye
    bound = jnp.max(jnp.sum(jnp.abs(system), axis=1, keepdims=True), axis=0, keepdims=True)
    scale = 2.0 / (bound + 2.0)
    r = (bound - 2.0) / (bound + 2.0)
    resid = eye - scale * system
    approx = scale * eye
    for step in range(SQUARINGS):
        s = 2.0 / (2.0 - r * r)
        if step == 0:
            approx = (s * scale) * (eye + resid)
            resid = (1.0 - s) * eye + s * matmul(resid, resid)
        elif step < SQUARINGS - 1:
            both = matmul(jnp.concatenate([approx, resid], axis=0), resid)
            approx = s * (approx + both[:n])
            resid = (1.0 - s) * eye + s * both[n:]
        else:
            approx = s * (approx + matmul(approx, resid))
        r = r * r / (2.0 - r * r)
    for _ in range(REFINES):
        resid = eye - matmul(approx, system)
        approx = approx + matmul(resid, approx)
    bands = lib.shape[0]
    high, low = split(matmul_nt(approx, lib))
    solve_ref[0, :, 0:bands] = high
    solve_ref[1, :, 0:bands] = low
    high, low = split(approx)
    solve_ref[0, :, bands:] = high
    solve_ref[1, :, bands:] = low
    high, low = split(lib)
    split_lib_ref[0] = high
    split_lib_ref[1] = low
    turned_ref[...] = jnp.zeros_like(turned_ref)
    turned_ref[0:n, :] = lib.T

    @pl.when(has_left)
    def _():
        for copy in heads:
            copy.wait_send()
        for copy in tails:
            copy.wait_recv()

    @pl.when(has_right)
    def _():
        for copy in tails:
            copy.wait_send()
        for copy in heads:
            copy.wait_recv()

    @pl.when(jnp.logical_not(has_left))
    def _():
        fill_left.wait()

    @pl.when(jnp.logical_not(has_right))
    def _():
        fill_right.wait()


def admm_kernel(
    padded_bands,
    spec_ref, left_ref, right_ref, aux_ref, solve_ref, split_lib_ref,
    abund_ref, sums_ref,
    s_ref, vw_ref, d1_ref, x_ref, near_v2_ref, d2_ref, e_ref, d4_ref, cv_ref, ch_ref,
    valid_ref, rinv_ref, lr_ref, near_ref, count_ref, below_ref, above_ref, far_ref, out_ref, load_sem, out_sem,
):
    bands, here = spec_ref.shape
    members = split_lib_ref.shape[2]
    side = left_ref.shape[1]
    wide = here + 2 * side
    loads = [
        pltpu.make_async_copy(src, s_ref.at[:, start : start + src.shape[1]], load_sem.at[k])
        for k, (src, start) in enumerate(((left_ref, 0), (spec_ref, side), (right_ref, side + here)))
    ]
    for load in loads:
        load.start()
    lane = lax.broadcasted_iota(jnp.int32, (8, LANES), 1)
    within = lane % ROWS
    below = (within < ROWS - 1).astype(jnp.float32)
    above = (within > 0).astype(jnp.float32)
    first_half = lane < ROWS
    tiles_all = wide // LANES

    def at(ref, i, rows=slice(0, 8)):
        return ref[rows, i * LANES : (i + 1) * LANES]

    segs = [jnp.broadcast_to(aux_ref[1:2, i * LANES : (i + 1) * LANES], (8, LANES)) for i in range(tiles_all)]
    rolled = [pltpu.roll(t, ROWS, 1) for t in segs]
    for i in range(tiles_all):
        right = jnp.where(first_half, rolled[i], rolled[min(i + 1, tiles_all - 1)])
        left = jnp.where(first_half, rolled[max(i - 1, 0)], rolled[i])
        lr = (right == segs[i]).astype(jnp.float32)
        ll = (left == segs[i]).astype(jnp.float32)
        sl = slice(i * LANES, (i + 1) * LANES)
        lr_ref[:, sl] = lr
        count = 1.0 / (1.0 + below + above + lr + ll)
        count_ref[:, sl] = count
        below_ref[:, sl] = count * below
        above_ref[:, sl] = count * above
        near_ref[:, sl] = count * jnp.where(first_half, lr, ll)
        far_ref[:, sl] = count * jnp.where(first_half, ll, lr)
        ok = jnp.broadcast_to(aux_ref[0:1, sl], (8, LANES))
        valid_ref[:, sl] = ok
        rinv_ref[:, sl] = 1.0 / (ok + penalty)

    for load in loads:
        load.wait()
    cut = smoothness / penalty
    thresh = sparsity / penalty

    for it in range(ITERS):
        final_turn = it == ITERS - 1
        lo = it * LANES
        span = wide - 2 * lo

        for start in range(lo, lo + span, CHUNK):
            cells = slice(start, start + CHUNK)
            spec = s_ref[:, cells]
            if it == 0:
                x = matmul_split(solve_ref, spec)
            else:
                x = matmul_split(solve_ref, vw_ref[:, cells])
            x_ref[:, cells] = x
            g = matmul_split(split_lib_ref, x)
            if it > 0:
                g = g - d1_ref[:, cells]
            v1 = (valid_ref[0:1, cells] * spec + penalty * g) * rinv_ref[0:1, cells]
            d1 = v1 - g
            if not final_turn:
                d1_ref[:, cells] = d1
            vw_ref[0:bands, cells] = v1 + d1

        first, last = lo // LANES, (wide - lo) // LANES

        def smooth_rows(b, carry, it=it, first=first, last=last, final_turn=final_turn):
            for part in range(ROW_BLOCK // 8):
                smooth_group(b * ROW_BLOCK + part * 8, it, first, last, final_turn)
            return carry

        def smooth_group(row, it, first, last, final_turn):
            rows = pl.ds(pl.multiple_of(row, 8), 8)
            wrows = pl.ds(pl.multiple_of(bands + row, 8), 8)

            def tile(ref, i):
                return ref[rows, i * LANES : (i + 1) * LANES]

            def put(ref, i, value):
                ref[rows, i * LANES : (i + 1) * LANES] = value

            def clamp(i):
                return min(max(i, first), last - 1)

            def half_rolled(field):
                return functools.cache(lambda i: pltpu.roll(field(i), ROWS, 1))

            def around(field, half, i):
                mine = field(i)
                total = at(below_ref, i) * pltpu.roll(mine, LANES - 1, 1)
                total += at(above_ref, i) * pltpu.roll(mine, 1, 1)
                total += at(near_ref, i) * half(i)
                far = jnp.where(first_half, half(clamp(i - 1)), half(clamp(i + 1)))
                return total + at(far_ref, i) * far

            @functools.cache
            def x(i):
                return tile(x_ref, i)

            @functools.cache
            def scaled(i):
                target = x(i) if it == 0 else x(i) + tile(e_ref, i)
                return target * at(count_ref, i)

            @functools.cache
            def once(i):
                if it == 0:
                    return scaled(i)
                return scaled(i) + tile(near_v2_ref, i)

            once_half = half_rolled(once)

            @functools.cache
            def twice(i):
                return scaled(i) + around(once, once_half, i)

            twice_half = half_rolled(twice)

            @functools.cache
            def edges(i):
                mine = twice(i)
                sv = below * (pltpu.roll(mine, LANES - 1, 1) - mine)
                sh = at(lr_ref, i) * (
                    jnp.where(first_half, twice_half(i), twice_half(clamp(i + 1))) - mine
                )
                if it > 0:
                    sv += tile(cv_ref, i)
                    sh += tile(ch_ref, i)
                cv = jnp.clip(sv, -cut, cut)
                ch = jnp.clip(sh, -cut, cut)
                return sv - 2.0 * cv, sh - 2.0 * ch, cv, ch

            dual_half = functools.cache(lambda i: pltpu.roll(edges(i)[1], ROWS, 1))

            for i in range(first, last):
                v2 = twice(i)
                d2 = v2 - x(i)
                if it > 0:
                    d2 += tile(d2_ref, i)
                part = x(i) if it == 0 else x(i) + tile(d4_ref, i)
                kept = jnp.minimum(part, thresh)
                vw_ref[wrows, i * LANES : (i + 1) * LANES] = (v2 + d2) + (part - 2.0 * kept)
                put(d4_ref, i, kept)
                if not final_turn:
                    wv, wh, cv, ch = edges(i)
                    across = jnp.where(first_half, dual_half(clamp(i - 1)), dual_half(i))
                    put(e_ref, i, (pltpu.roll(wv, 1, 1) - wv) + (across - wh) - d2)
                    put(d2_ref, i, d2)
                    put(cv_ref, i, cv)
                    put(ch_ref, i, ch)
                    put(near_v2_ref, i, around(twice, twice_half, i))

        lax.fori_loop(0, members // ROW_BLOCK, smooth_rows, 0)

    sums_ref[...] = jnp.zeros_like(sums_ref)
    stores = []
    for k in range(here // CHUNK):
        cells = slice(side + k * CHUNK, side + (k + 1) * CHUNK)
        out = slice(k * CHUNK, (k + 1) * CHUNK)
        x = matmul_split(solve_ref, vw_ref[:, cells])
        abund = jnp.maximum(x + d4_ref[:, cells] - thresh, 0.0)
        out_ref[:, out] = abund
        stores.append(pltpu.make_async_copy(out_ref.at[:, out], abund_ref.at[:, out], out_sem.at[k]))
        stores[k].start()
        masked = abund * valid_ref[0:1, cells]
        sums_ref[0:members, 0:bands] += matmul_nt_split(masked, s_ref[:, cells])
        sums_ref[0:members, padded_bands : padded_bands + members] += matmul_nt_split(masked, abund)
    for store in stores:
        store.wait()


def total_kernel(
    total_pixels, bands, members, per, groups,
    part_ref, lib_ref, turned_ref, out_ref,
    pair_ref, acc_ref, got_ref, rows_ref,
    pair_send, pair_recv, sum_send, sum_recv, row_send, row_recv, swap_send, swap_recv,
):
    me = lax.axis_index("pix")
    core = me % 2
    spot = me // 2
    half = per * groups
    wide = rows_ref.shape[1]
    partner = {"pix": spot * 2 + 1 - core}

    def peer(k):
        return {"pix": ((spot + k) % groups) * 2 + core}

    barrier = pltpu.get_barrier_semaphore()
    pl.semaphore_signal(barrier, inc=1, device_id=partner)
    for k in range(1, groups):
        pl.semaphore_signal(barrier, inc=1, device_id=peer(k))
    pl.semaphore_wait(barrier, groups)

    def block(k, of_core):
        place = of_core * half + ((spot + k) % groups) * per
        return pl.ds(pl.multiple_of(place, per), per)

    order = list(range(1, groups)) + [0]
    pair_copies = {}
    for k in order:
        pair_copies[k] = pltpu.make_async_remote_copy(
            part_ref.at[block(k, 1 - core)], pair_ref.at[k], pair_send.at[k], pair_recv.at[k],
            device_id=partner,
        )
        pair_copies[k].start()
    sum_copies = {}
    for k in order:
        pair_copies[k].wait_recv()
        acc_ref[k] = part_ref[block(k, core), :] + pair_ref[k]
        if k > 0:
            sum_copies[k] = pltpu.make_async_remote_copy(
                acc_ref.at[k], got_ref.at[k], sum_send.at[k], sum_recv.at[k], device_id=peer(k)
            )
            sum_copies[k].start()
    total = acc_ref[0]
    for k in range(1, groups):
        sum_copies[k].wait_recv()
        total += got_ref[k]
    total = total * (1.0 / total_pixels)
    mine = block(0, core)
    gram = total[:, wide : wide + members]
    denominator = matmul_nt(gram, lib_ref[...])
    rows_ref[mine, :] = jnp.zeros((per, wide), jnp.float32)
    rows_ref[mine, 0:bands] = (
        turned_ref[mine, :] * (total[:, 0:bands] + update_guard) / (denominator + update_guard)
    )
    row_copies = {}
    for k in range(1, groups):
        row_copies[k] = pltpu.make_async_remote_copy(
            rows_ref.at[mine], rows_ref.at[mine], row_send.at[k], row_recv.at[k], device_id=peer(k)
        )
        row_copies[k].start()
    swap_copies = {}
    for k in range(groups):
        if k > 0:
            row_copies[k].wait_recv()
        there = block(-k, core)
        swap_copies[k] = pltpu.make_async_remote_copy(
            rows_ref.at[there], rows_ref.at[there], swap_send.at[k], swap_recv.at[k],
            device_id=partner,
        )
        swap_copies[k].start()
    for k in range(groups):
        swap_copies[k].wait_recv()
    out_ref[...] = rows_ref[...].T[0:bands, 0:members]
    for k in range(groups):
        pair_copies[k].wait_send()
        swap_copies[k].wait_send()
        if k > 0:
            sum_copies[k].wait_send()
            row_copies[k].wait_send()


def on_device(spectra, library, segment_ids, valid_mask):
    peers = lax.axis_size("pix")
    bands, here = spectra.shape
    members = library.shape[1]
    side = HALO * ROWS
    wide = here + 2 * side
    groups = peers // 2
    per = 8 * pl.cdiv(members, 8 * peers)
    padded_bands = LANES * pl.cdiv(bands, LANES)
    padded = padded_bands + LANES * pl.cdiv(members, LANES)
    marked = jnp.repeat((segment_ids + 1).astype(jnp.float32), ROWS)
    aux = jnp.stack([valid_mask.astype(jnp.float32), marked] + [jnp.zeros_like(marked)] * 6)
    vmem = pl.BlockSpec(memory_space=pltpu.VMEM)
    hbm = pl.BlockSpec(memory_space=pltpu.HBM)
    edge = jax.ShapeDtypeStruct((bands, side), jnp.float32)
    solve, split_lib, turned, left, right, aux_wide = pl.pallas_call(
        functools.partial(start_kernel, peers),
        out_shape=(
            jax.ShapeDtypeStruct((2, members, bands + members), jnp.bfloat16),
            jax.ShapeDtypeStruct((2, bands, members), jnp.bfloat16),
            jax.ShapeDtypeStruct((per * peers, bands), jnp.float32),
            edge,
            edge,
            jax.ShapeDtypeStruct((8, wide), jnp.float32),
        ),
        in_specs=[vmem, hbm, vmem],
        out_specs=(vmem, vmem, vmem, hbm, hbm, vmem),
        scratch_shapes=[
            pltpu.SemaphoreType.DMA((4,)),
            pltpu.SemaphoreType.DMA((4,)),
            pltpu.SemaphoreType.DMA((2,)),
        ],
        compiler_params=pltpu.CompilerParams(collective_id=1, has_side_effects=True),
        name="start",
    )(library, spectra, aux)
    field = pltpu.VMEM((members, wide), jnp.float32)
    band_field = pltpu.VMEM((bands, wide), jnp.float32)
    line = pltpu.VMEM((8, wide), jnp.float32)
    stacked = pltpu.VMEM((bands + members, wide), jnp.float32)
    scratch = [band_field, stacked, band_field] + [field] * 7 + [line] * 8
    scratch += [
        pltpu.VMEM((members, here), jnp.float32),
        pltpu.SemaphoreType.DMA((3,)),
        pltpu.SemaphoreType.DMA((here // CHUNK,)),
    ]
    abundances, sums = pl.pallas_call(
        functools.partial(admm_kernel, padded_bands),
        out_shape=(
            jax.ShapeDtypeStruct((members, here), jnp.float32),
            jax.ShapeDtypeStruct((per * peers, padded), jnp.float32),
        ),
        in_specs=[hbm] * 3 + [vmem] * 3,
        out_specs=(hbm, vmem),
        scratch_shapes=scratch,
        compiler_params=pltpu.CompilerParams(vmem_limit_bytes=VMEM_LIMIT),
        name="admm",
    )(spectra, left, right, aux_wide, solve, split_lib)
    blocks = pltpu.VMEM((groups, per, padded), jnp.float32)
    new_library = pl.pallas_call(
        functools.partial(total_kernel, here * peers, bands, members, per, groups),
        out_shape=jax.ShapeDtypeStruct((bands, members), jnp.float32),
        in_specs=[vmem] * 3,
        out_specs=vmem,
        scratch_shapes=[blocks] * 3
        + [pltpu.VMEM((per * peers, padded_bands), jnp.float32)]
        + [pltpu.SemaphoreType.DMA((groups,))] * 8,
        compiler_params=pltpu.CompilerParams(collective_id=0, has_side_effects=True),
        name="total",
    )(sums, library, turned)
    return (abundances, new_library)


def solution(mesh):
    placed = (P(None, ("grp", "pix")), P(), P(("grp", "pix")), P(("grp", "pix")))
    return jax.shard_map(
        on_device,
        mesh=mesh,
        in_specs=placed,
        out_specs=(P(None, ("grp", "pix")), P("grp", None)),
        check_vma=False,
    )
```

```python
import functools

import jax
import jax.numpy as jnp
from jax import lax
from jax.experimental import pallas as pl
from jax.experimental.pallas import tpu as pltpu
from jax.sharding import PartitionSpec as P

ROWS = 64
ITERS = 3
SWEEPS = 2
HALO = 2 * ITERS
LANES = 128
CHUNK = 256
ROW_BLOCK = 8

penalty = 0.5
sparsity = 0.005
smoothness = 0.01
update_guard = 0.001
highest = lax.Precision.HIGHEST
SQUARINGS = 8
REFINES = 1
VMEM_LIMIT = 60000 * 1024


def matmul(a, b):
    return jnp.dot(a, b, precision=highest, preferred_element_type=jnp.float32)


def matmul_nt(a, b):
    return lax.dot_general(
        a, b, (((1,), (1,)), ((), ())), precision=highest, preferred_element_type=jnp.float32
    )


def matmul_tn(a, b):
    return lax.dot_general(
        a, b, (((0,), (0,)), ((), ())), precision=highest, preferred_element_type=jnp.float32
    )


def split(a):
    high = a.astype(jnp.bfloat16)
    return high, (a - high.astype(jnp.float32)).astype(jnp.bfloat16)


def matmul_split(a_ref, b):
    high, low = split(b)
    product = functools.partial(jnp.dot, preferred_element_type=jnp.float32)
    depth = b.shape[0]
    a_high, a_low = a_ref[0, :, 0:depth], a_ref[1, :, 0:depth]
    return product(a_high, high) + (product(a_high, low) + product(a_low, high))


def matmul_nt_split(a, b):
    contract = (((1,), (1,)), ((), ()))
    product = functools.partial(
        lax.dot_general, dimension_numbers=contract, preferred_element_type=jnp.float32
    )
    (a_high, a_low), (b_high, b_low) = split(a), split(b)
    return product(a_high, b_high) + (product(a_high, b_low) + product(a_low, b_high))


def start_kernel(
    peers,
    lib_ref, spec_ref, aux_ref,
    solve_ref, split_lib_ref, turned_ref, left_ref, right_ref, aux_wide_ref,
    send, recv, local,
):
    me = lax.axis_index("pix")
    here = spec_ref.shape[1]
    side = left_ref.shape[1]
    has_left, has_right = me > 0, me < peers - 1
    to_left, to_right = {"pix": me - 1}, {"pix": me + 1}

    barrier = pltpu.get_barrier_semaphore()

    @pl.when(has_left)
    def _():
        pl.semaphore_signal(barrier, inc=1, device_id=to_left)

    @pl.when(has_right)
    def _():
        pl.semaphore_signal(barrier, inc=1, device_id=to_right)

    pl.semaphore_wait(barrier, has_left.astype(jnp.int32) + has_right.astype(jnp.int32))

    heads = [
        pltpu.make_async_remote_copy(src, dst, send.at[k], recv.at[k], device_id=to_left)
        for k, (src, dst) in enumerate((
            (spec_ref.at[:, 0:side], right_ref),
            (aux_ref.at[:, 0:side], aux_wide_ref.at[:, side + here : here + 2 * side]),
        ))
    ]
    tails = [
        pltpu.make_async_remote_copy(src, dst, send.at[k + 2], recv.at[k + 2], device_id=to_right)
        for k, (src, dst) in enumerate((
            (spec_ref.at[:, here - side :], left_ref),
            (aux_ref.at[:, here - side :], aux_wide_ref.at[:, 0:side]),
        ))
    ]
    fill_left = pltpu.make_async_copy(spec_ref.at[:, 0:side], left_ref, local.at[0])
    fill_right = pltpu.make_async_copy(spec_ref.at[:, 0:side], right_ref, local.at[1])

    @pl.when(has_left)
    def _():
        for copy in heads:
            copy.start()

    @pl.when(has_right)
    def _():
        for copy in tails:
            copy.start()

    @pl.when(jnp.logical_not(has_left))
    def _():
        aux_wide_ref[:, 0:side] = jnp.zeros((8, side), jnp.float32)
        fill_left.start()

    @pl.when(jnp.logical_not(has_right))
    def _():
        aux_wide_ref[:, side + here :] = jnp.zeros((8, side), jnp.float32)
        fill_right.start()

    aux_wide_ref[:, side : side + here] = aux_ref[...]
    lib = lib_ref[...]
    n = lib.shape[1]
    rows = lax.broadcasted_iota(jnp.int32, (n, n), 0)
    cols = lax.broadcasted_iota(jnp.int32, (n, n), 1)
    eye = (rows == cols).astype(jnp.float32)
    system = matmul_tn(lib, lib) + 2.0 * eye
    bound = jnp.max(jnp.sum(jnp.abs(system), axis=1, keepdims=True), axis=0, keepdims=True)
    scale = 2.0 / (bound + 2.0)
    r = (bound - 2.0) / (bound + 2.0)
    resid = eye - scale * system
    approx = scale * eye
    for step in range(SQUARINGS):
        s = 2.0 / (2.0 - r * r)
        if step == 0:
            approx = (s * scale) * (eye + resid)
            resid = (1.0 - s) * eye + s * matmul(resid, resid)
        elif step < SQUARINGS - 1:
            both = matmul(jnp.concatenate([approx, resid], axis=0), resid)
            approx = s * (approx + both[:n])
            resid = (1.0 - s) * eye + s * both[n:]
        else:
            approx = s * (approx + matmul(approx, resid))
        r = r * r / (2.0 - r * r)
    for _ in range(REFINES):
        resid = eye - matmul(approx, system)
        approx = approx + matmul(resid, approx)
    bands = lib.shape[0]
    high, low = split(matmul_nt(approx, lib))
    solve_ref[0, :, 0:bands] = high
    solve_ref[1, :, 0:bands] = low
    high, low = split(approx)
    solve_ref[0, :, bands:] = high
    solve_ref[1, :, bands:] = low
    high, low = split(lib)
    split_lib_ref[0] = high
    split_lib_ref[1] = low
    turned_ref[...] = jnp.zeros_like(turned_ref)
    turned_ref[0:n, :] = lib.T

    @pl.when(has_left)
    def _():
        for copy in heads:
            copy.wait_send()
        for copy in tails:
            copy.wait_recv()

    @pl.when(has_right)
    def _():
        for copy in tails:
            copy.wait_send()
        for copy in heads:
            copy.wait_recv()

    @pl.when(jnp.logical_not(has_left))
    def _():
        fill_left.wait()

    @pl.when(jnp.logical_not(has_right))
    def _():
        fill_right.wait()


def admm_kernel(
    padded_bands,
    spec_ref, left_ref, right_ref, aux_ref, solve_ref, split_lib_ref,
    abund_ref, sums_ref,
    s_ref, vw_ref, d1_ref, x_ref, near_v2_ref, d2_ref, e_ref, d4_ref, cv_ref, ch_ref, cu_ref, cl_ref,
    valid_ref, rinv_ref, lr_ref, ll_ref, near_ref, count_ref, below_ref, above_ref, far_ref, out_ref, load_sem, out_sem,
):
    bands, here = spec_ref.shape
    members = split_lib_ref.shape[2]
    side = left_ref.shape[1]
    wide = here + 2 * side
    loads = [
        pltpu.make_async_copy(src, s_ref.at[:, start : start + src.shape[1]], load_sem.at[k])
        for k, (src, start) in enumerate(((left_ref, 0), (spec_ref, side), (right_ref, side + here)))
    ]
    for load in loads:
        load.start()
    lane = lax.broadcasted_iota(jnp.int32, (8, LANES), 1)
    within = lane % ROWS
    below = (within < ROWS - 1).astype(jnp.float32)
    above = (within > 0).astype(jnp.float32)
    first_half = lane < ROWS
    tiles_all = wide // LANES

    def at(ref, i, rows=slice(0, 8)):
        return ref[rows, i * LANES : (i + 1) * LANES]

    segs = [jnp.broadcast_to(aux_ref[1:2, i * LANES : (i + 1) * LANES], (8, LANES)) for i in range(tiles_all)]
    rolled = [pltpu.roll(t, ROWS, 1) for t in segs]
    for i in range(tiles_all):
        right = jnp.where(first_half, rolled[i], rolled[min(i + 1, tiles_all - 1)])
        left = jnp.where(first_half, rolled[max(i - 1, 0)], rolled[i])
        lr = (right == segs[i]).astype(jnp.float32)
        ll = (left == segs[i]).astype(jnp.float32)
        sl = slice(i * LANES, (i + 1) * LANES)
        lr_ref[:, sl] = lr
        ll_ref[:, sl] = ll
        count = 1.0 / (1.0 + below + above + lr + ll)
        count_ref[:, sl] = count
        below_ref[:, sl] = count * below
        above_ref[:, sl] = count * above
        near_ref[:, sl] = count * jnp.where(first_half, lr, ll)
        far_ref[:, sl] = count * jnp.where(first_half, ll, lr)
        ok = jnp.broadcast_to(aux_ref[0:1, sl], (8, LANES))
        valid_ref[:, sl] = ok
        rinv_ref[:, sl] = 1.0 / (ok + penalty)

    for load in loads:
        load.wait()
    cut = smoothness / penalty
    thresh = sparsity / penalty

    for it in range(ITERS):
        final_turn = it == ITERS - 1
        lo = it * LANES
        span = wide - 2 * lo

        for start in range(lo, lo + span, CHUNK):
            cells = slice(start, start + CHUNK)
            spec = s_ref[:, cells]
            if it == 0:
                x = matmul_split(solve_ref, spec)
            else:
                x = matmul_split(solve_ref, vw_ref[:, cells])
            x_ref[:, cells] = x
            g = matmul_split(split_lib_ref, x)
            if it > 0:
                g = g - d1_ref[:, cells]
            v1 = (valid_ref[0:1, cells] * spec + penalty * g) * rinv_ref[0:1, cells]
            d1 = v1 - g
            if not final_turn:
                d1_ref[:, cells] = d1
            vw_ref[0:bands, cells] = v1 + d1

        first, last = lo // LANES, (wide - lo) // LANES

        def smooth_rows(b, carry, it=it, first=first, last=last, final_turn=final_turn):
            for part in range(ROW_BLOCK // 8):
                smooth_group(b * ROW_BLOCK + part * 8, it, first, last, final_turn)
            return carry

        def smooth_group(row, it, first, last, final_turn):
            rows = pl.ds(pl.multiple_of(row, 8), 8)
            wrows = pl.ds(pl.multiple_of(bands + row, 8), 8)

            def tile(ref, i):
                return ref[rows, i * LANES : (i + 1) * LANES]

            def put(ref, i, value):
                ref[rows, i * LANES : (i + 1) * LANES] = value

            def clamp(i):
                return min(max(i, first), last - 1)

            def half_rolled(field):
                return functools.cache(lambda i: pltpu.roll(field(i), ROWS, 1))

            def turned(field, by):
                return functools.cache(lambda i: pltpu.roll(field(i), by, 1))

            def around(up, down, half, i):
                total = at(below_ref, i) * up(i) + at(above_ref, i) * down(i)
                total += at(near_ref, i) * half(i)
                far = jnp.where(first_half, half(clamp(i - 1)), half(clamp(i + 1)))
                return total + at(far_ref, i) * far

            @functools.cache
            def x(i):
                return tile(x_ref, i)

            @functools.cache
            def scaled(i):
                target = x(i) if it == 0 else x(i) + tile(e_ref, i)
                return target * at(count_ref, i)

            @functools.cache
            def once(i):
                if it == 0:
                    return scaled(i)
                return scaled(i) + tile(near_v2_ref, i)

            once_half = half_rolled(once)
            once_up, once_down = turned(once, LANES - 1), turned(once, 1)

            @functools.cache
            def twice(i):
                return scaled(i) + around(once_up, once_down, once_half, i)

            twice_half = half_rolled(twice)
            twice_up, twice_down = turned(twice, LANES - 1), turned(twice, 1)

            def dual(change, clip_ref, i):
                total = change if it == 0 else change + tile(clip_ref, i)
                clipped = jnp.clip(total, -cut, cut)
                if it < ITERS - 2:
                    put(clip_ref, i, clipped)
                return total - 2.0 * clipped

            def adjoint(i):
                mine = twice(i)
                right = jnp.where(first_half, twice_half(i), twice_half(clamp(i + 1)))
                left = jnp.where(first_half, twice_half(clamp(i - 1)), twice_half(i))
                from_above = dual(above * (mine - twice_down(i)), cu_ref, i)
                own_below = dual(below * (twice_up(i) - mine), cv_ref, i)
                from_left = dual(at(ll_ref, i) * (mine - left), cl_ref, i)
                own_right = dual(at(lr_ref, i) * (right - mine), ch_ref, i)
                return (from_above - own_below) + (from_left - own_right)

            for i in range(first, last):
                v2 = twice(i)
                d2 = v2 - x(i)
                if it > 0:
                    d2 += tile(d2_ref, i)
                part = x(i) if it == 0 else x(i) + tile(d4_ref, i)
                kept = jnp.minimum(part, thresh)
                vw_ref[wrows, i * LANES : (i + 1) * LANES] = (v2 + d2) + (part - 2.0 * kept)
                put(d4_ref, i, kept)
                if not final_turn:
                    put(e_ref, i, adjoint(i) - d2)
                    put(d2_ref, i, d2)
                    put(near_v2_ref, i, around(twice_up, twice_down, twice_half, i))

        lax.fori_loop(0, members // ROW_BLOCK, smooth_rows, 0)

    sums_ref[...] = jnp.zeros_like(sums_ref)
    stores = []
    for k in range(here // CHUNK):
        cells = slice(side + k * CHUNK, side + (k + 1) * CHUNK)
        out = slice(k * CHUNK, (k + 1) * CHUNK)
        x = matmul_split(solve_ref, vw_ref[:, cells])
        abund = jnp.maximum(x + d4_ref[:, cells] - thresh, 0.0)
        out_ref[:, out] = abund
        stores.append(pltpu.make_async_copy(out_ref.at[:, out], abund_ref.at[:, out], out_sem.at[k]))
        stores[k].start()
        masked = abund * valid_ref[0:1, cells]
        sums_ref[0:members, 0:bands] += matmul_nt_split(masked, s_ref[:, cells])
        sums_ref[0:members, padded_bands : padded_bands + members] += matmul_nt_split(masked, abund)
    for store in stores:
        store.wait()


def total_kernel(
    total_pixels, bands, members, per, groups,
    part_ref, lib_ref, turned_ref, out_ref,
    pair_ref, acc_ref, got_ref, rows_ref,
    pair_send, pair_recv, sum_send, sum_recv, row_send, row_recv, swap_send, swap_recv,
):
    me = lax.axis_index("pix")
    core = me % 2
    spot = me // 2
    half = per * groups
    wide = rows_ref.shape[1]
    partner = {"pix": spot * 2 + 1 - core}

    def peer(k):
        return {"pix": ((spot + k) % groups) * 2 + core}

    barrier = pltpu.get_barrier_semaphore()
    pl.semaphore_signal(barrier, inc=1, device_id=partner)
    for k in range(1, groups):
        pl.semaphore_signal(barrier, inc=1, device_id=peer(k))
    pl.semaphore_wait(barrier, groups)

    def block(k, of_core):
        place = of_core * half + ((spot + k) % groups) * per
        return pl.ds(pl.multiple_of(place, per), per)

    order = list(range(1, groups)) + [0]
    pair_copies = {}
    for k in order:
        pair_copies[k] = pltpu.make_async_remote_copy(
            part_ref.at[block(k, 1 - core)], pair_ref.at[k], pair_send.at[k], pair_recv.at[k],
            device_id=partner,
        )
        pair_copies[k].start()
    sum_copies = {}
    for k in order:
        pair_copies[k].wait_recv()
        acc_ref[k] = part_ref[block(k, core), :] + pair_ref[k]
        if k > 0:
            sum_copies[k] = pltpu.make_async_remote_copy(
                acc_ref.at[k], got_ref.at[k], sum_send.at[k], sum_recv.at[k], device_id=peer(k)
            )
            sum_copies[k].start()
    total = acc_ref[0]
    for k in range(1, groups):
        sum_copies[k].wait_recv()
        total += got_ref[k]
    total = total * (1.0 / total_pixels)
    mine = block(0, core)
    gram = total[:, wide : wide + members]
    denominator = matmul_nt(gram, lib_ref[...])
    rows_ref[mine, :] = jnp.zeros((per, wide), jnp.float32)
    rows_ref[mine, 0:bands] = (
        turned_ref[mine, :] * (total[:, 0:bands] + update_guard) / (denominator + update_guard)
    )
    row_copies = {}
    for k in range(1, groups):
        row_copies[k] = pltpu.make_async_remote_copy(
            rows_ref.at[mine], rows_ref.at[mine], row_send.at[k], row_recv.at[k], device_id=peer(k)
        )
        row_copies[k].start()
    swap_copies = {}
    for k in range(groups):
        if k > 0:
            row_copies[k].wait_recv()
        there = block(-k, core)
        swap_copies[k] = pltpu.make_async_remote_copy(
            rows_ref.at[there], rows_ref.at[there], swap_send.at[k], swap_recv.at[k],
            device_id=partner,
        )
        swap_copies[k].start()
    for k in range(groups):
        swap_copies[k].wait_recv()
    out_ref[...] = rows_ref[...].T[0:bands, 0:members]
    for k in range(groups):
        pair_copies[k].wait_send()
        swap_copies[k].wait_send()
        if k > 0:
            sum_copies[k].wait_send()
            row_copies[k].wait_send()


def on_device(spectra, library, segment_ids, valid_mask):
    peers = lax.axis_size("pix")
    bands, here = spectra.shape
    members = library.shape[1]
    side = HALO * ROWS
    wide = here + 2 * side
    groups = peers // 2
    per = 8 * pl.cdiv(members, 8 * peers)
    padded_bands = LANES * pl.cdiv(bands, LANES)
    padded = padded_bands + LANES * pl.cdiv(members, LANES)
    marked = jnp.repeat((segment_ids + 1).astype(jnp.float32), ROWS)
    aux = jnp.stack([valid_mask.astype(jnp.float32), marked] + [jnp.zeros_like(marked)] * 6)
    vmem = pl.BlockSpec(memory_space=pltpu.VMEM)
    hbm = pl.BlockSpec(memory_space=pltpu.HBM)
    edge = jax.ShapeDtypeStruct((bands, side), jnp.float32)
    solve, split_lib, turned, left, right, aux_wide = pl.pallas_call(
        functools.partial(start_kernel, peers),
        out_shape=(
            jax.ShapeDtypeStruct((2, members, bands + members), jnp.bfloat16),
            jax.ShapeDtypeStruct((2, bands, members), jnp.bfloat16),
            jax.ShapeDtypeStruct((per * peers, bands), jnp.float32),
            edge,
            edge,
            jax.ShapeDtypeStruct((8, wide), jnp.float32),
        ),
        in_specs=[vmem, hbm, vmem],
        out_specs=(vmem, vmem, vmem, hbm, hbm, vmem),
        scratch_shapes=[
            pltpu.SemaphoreType.DMA((4,)),
            pltpu.SemaphoreType.DMA((4,)),
            pltpu.SemaphoreType.DMA((2,)),
        ],
        compiler_params=pltpu.CompilerParams(collective_id=1, has_side_effects=True),
        name="start",
    )(library, spectra, aux)
    field = pltpu.VMEM((members, wide), jnp.float32)
    band_field = pltpu.VMEM((bands, wide), jnp.float32)
    line = pltpu.VMEM((8, wide), jnp.float32)
    stacked = pltpu.VMEM((bands + members, wide), jnp.float32)
    scratch = [band_field, stacked, band_field] + [field] * 9 + [line] * 9
    scratch += [
        pltpu.VMEM((members, here), jnp.float32),
        pltpu.SemaphoreType.DMA((3,)),
        pltpu.SemaphoreType.DMA((here // CHUNK,)),
    ]
    abundances, sums = pl.pallas_call(
        functools.partial(admm_kernel, padded_bands),
        out_shape=(
            jax.ShapeDtypeStruct((members, here), jnp.float32),
            jax.ShapeDtypeStruct((per * peers, padded), jnp.float32),
        ),
        in_specs=[hbm] * 3 + [vmem] * 3,
        out_specs=(hbm, vmem),
        scratch_shapes=scratch,
        compiler_params=pltpu.CompilerParams(vmem_limit_bytes=VMEM_LIMIT),
        name="admm",
    )(spectra, left, right, aux_wide, solve, split_lib)
    blocks = pltpu.VMEM((groups, per, padded), jnp.float32)
    new_library = pl.pallas_call(
        functools.partial(total_kernel, here * peers, bands, members, per, groups),
        out_shape=jax.ShapeDtypeStruct((bands, members), jnp.float32),
        in_specs=[vmem] * 3,
        out_specs=vmem,
        scratch_shapes=[blocks] * 3
        + [pltpu.VMEM((per * peers, padded_bands), jnp.float32)]
        + [pltpu.SemaphoreType.DMA((groups,))] * 8,
        compiler_params=pltpu.CompilerParams(collective_id=0, has_side_effects=True),
        name="total",
    )(sums, library, turned)
    return (abundances, new_library)


def solution(mesh):
    placed = (P(None, ("grp", "pix")), P(), P(("grp", "pix")), P(("grp", "pix")))
    return jax.shard_map(
        on_device,
        mesh=mesh,
        in_specs=placed,
        out_specs=(P(None, ("grp", "pix")), P("grp", None)),
        check_vma=False,
    )
```
